128 devices in a mesh: row: 8 (over x, y_lo), col: 8 (over z, core), band: 2 (over y_hi).
Axes of the slice: x: 4, y: 4 (y_hi: 2, y_lo: 2; y = y_hi * 2 + y_lo), z: 4, core: 2. Of those that a mesh axis runs over, the one named last changes fastest.
Arguments:
- freq_index: int32 [2], replicated, may hold values from 0 to 32
- band_energy: float32 [16], replicated, may hold values from -4 to 4
- pole_amp: float32 [8192, 8192], P('row', 'col'), may hold values from -6 to 6
- pole_freq: float32 [8192, 8192], P('row', 'col'), may hold values from 0.5 to 4
- left_pieces: bfloat16 [16, 256, 8192], P(('col', 'band'), None, 'row'), may hold values from -0.032958984 to 0.032958984
- right_pieces: bfloat16 [16, 256, 8192], P(('row', 'band'), None, 'col'), may hold values from -0.032958984 to 0.032958984
Outputs:
- sigma: float32 [2, 256, 256], P(None, ('row', 'col', 'band'))
The draws below stay inside these ranges and needn't reach their ends.
All inputs are finite; a program needn't handle non-finite values.
Results may differ from the reference program's by a relative error of at most 0.0055.
Values may be sent and summed in bfloat16 or wider, within the bound.
A program may use at most 128 MiB of HBM per device.

```python
import math
import jax
import jax.numpy as jnp
from jax import lax

TILE = 1024
NSTATE = 256
NW = 2
NG = 8192
BANDS = 16


def level_of(rng, dims, split, smallest, high):
    gain = 1.0
    for axis_at, blocks in split:
        heights = jax.random.uniform(jax.random.fold_in(jax.random.fold_in(rng, 6), axis_at), (blocks,), jnp.float32, smallest / len(split), high / len(split))
        gain = gain * jnp.repeat(jnp.exp(heights), dims[axis_at] // blocks).reshape((-1,) + (1,) * (len(dims) - 1 - axis_at))
    return gain


def normal_values(key, shape, scale, bound, split=(), dtype=jnp.bfloat16):
    result = scale * jax.random.normal(key, shape, jnp.float32)
    if split:
        result = result * level_of(key, shape, split, -0.22, 0.18)
    return jnp.clip(result, -bound, bound).astype(dtype)


def setup_inputs(seed: int = 0) -> dict:
    arg_keys = jax.random.split(jax.random.key(seed), 7)
    freq_index = jax.random.randint(arg_keys[0], (NW,), 0, 33).astype(jnp.int32)
    band_energy = jnp.clip(jax.random.uniform(arg_keys[1], (BANDS,), jnp.float32, -4.0, 4.0), -4.0, 4.0)
    pole_amp = normal_values(arg_keys[2], (NG, NG), 1.0, 6.0, ((0, 8), (1, 8)), jnp.float32)
    pole_freq = jnp.clip(jnp.exp(math.log(4.0) - 2.0794415 * jax.random.uniform(arg_keys[3], (NG, NG), jnp.float32) ** level_of(arg_keys[3], (NG, NG), ((0, 8), (1, 8)), -0.2, 0.2)), 0.5, 4.0)
    left_pieces = normal_values(arg_keys[4], (BANDS, NSTATE, NG), (1.0 / (NG ** 0.5 * BANDS ** 0.25)), 0.032958984, ((0, 16), (2, 8)))
    right_pieces = normal_values(arg_keys[5], (BANDS, NSTATE, NG), (1.0 / (NG ** 0.5 * BANDS ** 0.25)), 0.032958984, ((0, 16), (2, 8)))
    return dict(freq_index=freq_index, band_energy=band_energy, pole_amp=pole_amp, pole_freq=pole_freq, left_pieces=left_pieces, right_pieces=right_pieces)


def reference(freq_index, band_energy, pole_amp, pole_freq, left_pieces, right_pieces):
    freq = -4.0 + 0.25 * freq_index.astype(jnp.float32)
    nblock = NG // TILE

    def one_band(total, items):
        energy, left_band, right_band = items
        left_blocks = left_band.astype(jnp.float32).reshape(NSTATE, nblock, TILE)
        right_blocks = right_band.astype(jnp.float32).reshape(NSTATE, nblock, TILE)
        results = []
        for w in range(NW):
            distance = freq[w] - energy - pole_freq
            screened = (pole_amp * distance / (distance * distance + 0.25)).astype(jnp.bfloat16)
            blocks = screened.astype(jnp.float32).reshape(nblock, TILE, nblock, TILE)
            partial_value = jnp.einsum("nrg,rgch->nrch", left_blocks, blocks).astype(jnp.bfloat16)
            results.append(jnp.einsum("nrch,mch->nm", partial_value.astype(jnp.float32), right_blocks))
        return total + jnp.stack(results), None

    start = jnp.zeros((NW, NSTATE, NSTATE), jnp.float32)
    sigma, unused = lax.scan(one_band, start, (band_energy, left_pieces, right_pieces))
    return sigma
```

```python
import jax
import jax.numpy as jnp
from jax import lax
from jax.experimental import pallas as pl
from jax.experimental.pallas import tpu as pltpu
from jax.sharding import PartitionSpec as P

MESH = pl.DeviceIdType.MESH
F32 = jnp.float32
BF16 = jnp.bfloat16

NST = 256
TILE = 1024
HALF = NST // 2
CHUNK = 512
NCHUNK = TILE // CHUNK
LANES = 128


def kernel(freq_index, band_energy, pole_freq, pole_amp, left, right, out,
           pf, pa, lbuf, rbuf, ubuf, sig, tiles, in_a, vx, in_x, vy, in_y, vz, in_z,
           load_sem, own_sem, lsend, lrecv, rsend, rrecv, ssend, srecv):
    row, col, yhi = lax.axis_index("row"), lax.axis_index("col"), lax.axis_index("band")
    x, ylo, z, core = row // 2, row % 2, col // 2, col % 2
    y = yhi * 2 + ylo

    def device(dx=0, dy=0, dz=0, dc=0, flip=0):
        yy = (y + dy) % 4
        return {
            "row": ((x + dx) % 4) * 2 + (yy % 2 + flip) % 2,
            "col": ((z + dz) % 4) * 2 + (core + dc) % 2,
            "band": yy // 2,
        }

    def pole_copies(c):
        cs = pl.ds(pl.multiple_of(c * CHUNK, CHUNK), CHUNK)
        return (
            pltpu.make_async_copy(pole_freq.at[:, cs], pf.at[:, cs], load_sem.at[c]),
            pltpu.make_async_copy(pole_amp.at[:, cs], pa.at[:, cs], load_sem.at[NCHUNK + c]),
        )

    own_l = pltpu.make_async_copy(left.at[0], lbuf.at[0], own_sem.at[0])
    own_r = pltpu.make_async_copy(right.at[0], rbuf.at[0], own_sem.at[1])
    own_l.start()
    for c in range(NCHUNK):
        for copy in pole_copies(c):
            copy.start()
    own_r.start()

    barrier = pltpu.get_barrier_semaphore()
    peers = [device(dc=1)]
    for k in (1, 2, 3):
        peers += [device(dx=k), device(dy=k), device(dz=k)]
    for peer in peers:
        pl.semaphore_signal(barrier, inc=1, device_id=peer, device_id_type=MESH)
    pl.semaphore_wait(barrier, len(peers))

    started = []

    def send(src, dst, send_sem, recv_sem, to):
        copy = pltpu.make_async_remote_copy(
            src_ref=src, dst_ref=dst, send_sem=send_sem, recv_sem=recv_sem,
            device_id=to, device_id_type=MESH,
        )
        copy.start()
        started.append(copy)
        return copy

    lo, hi = pl.ds(0, HALF), pl.ds(HALF, HALF)

    l_c1 = send(left.at[0], lbuf.at[1], lsend.at[0], lrecv.at[0], device(dc=1))
    r_y1 = send(right.at[0], rbuf.at[1], rsend.at[0], rrecv.at[0], device(flip=1))
    l_zm = send(left.at[0], lbuf.at[6], lsend.at[1], lrecv.at[1], device(dz=1))
    l_zp = send(left.at[0], lbuf.at[2], lsend.at[2], lrecv.at[2], device(dz=3))
    r_xm = send(right.at[0], rbuf.at[6], rsend.at[1], rrecv.at[1], device(dx=1))
    r_xp = send(right.at[0], rbuf.at[2], rsend.at[2], rrecv.at[2], device(dx=3))

    def scalars(slot):
        zs, cs = (z + slot // 2) % 4, (core + slot) % 2
        energy = band_energy[(zs * 2 + cs) * 2 + yhi]
        return [-4.0 + 0.25 * freq_index[w].astype(F32) - energy for w in range(2)]

    def first(slot, c):
        cs = pl.ds(pl.multiple_of(c * CHUNK, CHUNK), CHUNK)
        shifts = scalars(slot)
        for w in range(2):
            d = shifts[w] - pf[:, cs]
            screened = (pa[:, cs] * d / (d * d + 0.25)).astype(BF16)
            ubuf[slot, pl.ds(w * NST, NST), cs] = jnp.dot(
                lbuf[slot], screened, preferred_element_type=F32
            ).astype(BF16)

    def first_loop(count, slot_of, loads=False):
        def step(i, carry):
            c = i % NCHUNK
            if loads:
                @pl.when(i < NCHUNK)
                def _():
                    for copy in pole_copies(c):
                        copy.wait()
            first(slot_of(i // NCHUNK), c)
            return carry

        lax.fori_loop(0, count * NCHUNK, step, 0)

    def second(rslot):
        xs, ys = (x + rslot // 2) % 4, (ylo + rslot) % 2
        uslot = ((xs - z + 4) % 4) * 2 + (ys + core) % 2
        term = lax.dot_general(
            ubuf[uslot], rbuf[rslot], (((1,), (1,)), ((), ())), preferred_element_type=F32
        )
        for h in range(2):
            sig[pl.ds(h * 2 * NST, 2 * NST), :] += term[:, h * LANES:(h + 1) * LANES]

    def second_loop(count, slot_of):
        def step(i, carry):
            second(slot_of(i))
            return carry

        lax.fori_loop(0, count, step, 0)

    sig[...] = jnp.zeros_like(sig)
    own_l.wait()
    l_c1.wait_recv()
    first_loop(2, lambda i: i, loads=True)

    l_zm.wait_recv()
    a1 = send(lbuf.at[6, lo], lbuf.at[4, lo], lsend.at[3], lrecv.at[3], device(dz=1))
    a2 = send(lbuf.at[6], lbuf.at[7], lsend.at[4], lrecv.at[4], device(dc=1))
    l_zp.wait_recv()
    a3 = send(lbuf.at[2, hi], lbuf.at[4, hi], lsend.at[5], lrecv.at[5], device(dz=3))
    a4 = send(lbuf.at[2], lbuf.at[3], lsend.at[6], lrecv.at[6], device(dc=1))
    r_xm.wait_recv()
    b1 = send(rbuf.at[6, lo], rbuf.at[4, lo], rsend.at[3], rrecv.at[3], device(dx=1))
    r_xp.wait_recv()
    b2 = send(rbuf.at[2, hi], rbuf.at[4, hi], rsend.at[4], rrecv.at[4], device(dx=3))
    r_y1.wait_recv()
    b3 = send(rbuf.at[1], rbuf.at[7], rsend.at[5], rrecv.at[5], device(dx=1))
    b4 = send(rbuf.at[1], rbuf.at[3], rsend.at[6], rrecv.at[6], device(dx=3))

    first_loop(2, lambda i: 6 - 4 * i)
    a1.wait_recv()
    a3.wait_recv()
    a5 = send(lbuf.at[4], lbuf.at[5], lsend.at[7], lrecv.at[7], device(dc=1))
    b1.wait_recv()
    b2.wait_recv()
    b5 = send(rbuf.at[4], rbuf.at[5], rsend.at[7], rrecv.at[7], device(flip=1))
    a2.wait_recv()
    a4.wait_recv()
    first_loop(2, lambda i: 7 - 4 * i)
    a5.wait_recv()
    first_loop(2, lambda i: 4 + i)

    own_r.wait()
    second_loop(2, lambda i: i)
    second_loop(3, lambda i: 2 + 2 * i)
    b3.wait_recv()
    b4.wait_recv()
    b5.wait_recv()
    second_loop(3, lambda i: 3 + 2 * i)

    def build(t, carry):
        dc, dx, dy, dz = t // 64, (t // 16) % 4, (t // 4) % 4, t % 4
        xx, yy, zz, cc = (x + dx) % 4, (y + dy) % 4, (z + dz) % 4, (core + dc) % 2
        owner = ((((xx * 2 + yy % 2) * 4 + zz) * 2 + cc) * 2) + yy // 2
        for r in range(2):
            tiles[t, pl.ds(4 * r, 4), :] = sig[pl.ds(owner * 2 + r, 4, stride=NST), :]
        return carry

    lax.fori_loop(64, 128, build, 0)
    s = send(tiles.at[pl.ds(64, 64)], in_a, ssend.at[0], srecv.at[0], device(dc=1))
    lax.fori_loop(0, 64, build, 0)
    s.wait_recv()
    vx[...] = tiles[pl.ds(0, 64)] + in_a[...]

    def stage(value, landing, at, shift):
        n = landing.shape[1]
        copies = [
            send(value.at[pl.ds(k * n, n)], landing.at[k - 1], ssend.at[at + k], srecv.at[at + k], shift(k))
            for k in (2, 1, 3)
        ]
        total = value[pl.ds(0, n)]
        for copy in copies:
            copy.wait_recv()
        for k in range(3):
            total = total + landing[k]
        return total

    vy[...] = stage(vx, in_x, 0, lambda k: device(dx=k))
    vz[...] = stage(vy, in_y, 3, lambda k: device(dy=k))
    out[...] = stage(vz, in_z, 6, lambda k: device(dz=k))[0]
    for copy in started:
        copy.wait_send()


def body(freq_index, band_energy, pole_amp, pole_freq, left_pieces, right_pieces):
    smem = pl.BlockSpec(memory_space=pltpu.SMEM)
    anywhere = pl.BlockSpec(memory_space=pl.ANY)
    tile = (8, LANES)
    dma = pltpu.SemaphoreType.DMA
    result = pl.pallas_call(
        kernel,
        out_shape=jax.ShapeDtypeStruct(tile, F32),
        in_specs=[smem, smem, anywhere, anywhere, anywhere, anywhere],
        out_specs=pl.BlockSpec(memory_space=pltpu.VMEM),
        scratch_shapes=[
            pltpu.VMEM((TILE, TILE), F32),
            pltpu.VMEM((TILE, TILE), F32),
            pltpu.VMEM((8, NST, TILE), BF16),
            pltpu.VMEM((8, NST, TILE), BF16),
            pltpu.VMEM((8, 2 * NST, TILE), BF16),
            pltpu.VMEM((4 * NST, LANES), F32),
            pltpu.VMEM((128,) + tile, F32),
            pltpu.VMEM((64,) + tile, F32),
            pltpu.VMEM((64,) + tile, F32),
            pltpu.VMEM((3, 16) + tile, F32),
            pltpu.VMEM((16,) + tile, F32),
            pltpu.VMEM((3, 4) + tile, F32),
            pltpu.VMEM((4,) + tile, F32),
            pltpu.VMEM((3, 1) + tile, F32),
            dma((2 * NCHUNK,)), dma((2,)),
            dma((8,)), dma((8,)), dma((8,)), dma((8,)), dma((10,)), dma((10,)),
        ],
        compiler_params=pltpu.CompilerParams(
            collective_id=0, has_side_effects=True, vmem_limit_bytes=56 << 20
        ),
        name="self_energy",
    )(freq_index, band_energy, pole_freq, pole_amp, left_pieces, right_pieces)
    return result.reshape(2, 2, 2, LANES).transpose(2, 0, 1, 3).reshape(2, 2, 2 * LANES)


def solution(mesh):
    in_specs = (
        P(),
        P(),
        P("row", "col"),
        P("row", "col"),
        P(("col", "band"), None, "row"),
        P(("row", "band"), None, "col"),
    )
    out_specs = P(None, ("row", "col", "band"), None)
    return jax.shard_map(body, mesh=mesh, in_specs=in_specs, out_specs=out_specs, check_vma=False)
```

```python
import jax
import jax.numpy as jnp
from jax import lax
from jax.experimental import pallas as pl
from jax.experimental.pallas import tpu as pltpu
from jax.sharding import PartitionSpec as P

MESH = pl.DeviceIdType.MESH
F32 = jnp.float32
BF16 = jnp.bfloat16

NST = 256
TILE = 1024
HALF = NST // 2
CHUNK = 512
NCHUNK = TILE // CHUNK
SHARE = 32
LANES = 128


def kernel(freq_hbm, energy_hbm, pole_freq, pole_amp, left, right, out,
           freq_index, band_energy, pf, pa, lbuf, rbuf, ubuf, sig, tiles, in_a, total, in_f,
           load_sem, own_sem, lsend, lrecv, rsend, rrecv, ssend, srecv, plane_sem, all_sem):
    row, col, yhi = lax.axis_index("row"), lax.axis_index("col"), lax.axis_index("band")
    x, ylo, z, core = row // 2, row % 2, col // 2, col % 2
    y = yhi * 2 + ylo

    def device(dx=0, dy=0, dz=0, dc=0, flip=0):
        yy = (y + dy) % 4
        return {
            "row": ((x + dx) % 4) * 2 + (yy % 2 + flip) % 2,
            "col": ((z + dz) % 4) * 2 + (core + dc) % 2,
            "band": yy // 2,
        }

    def pole_copies(c):
        cs = pl.ds(pl.multiple_of(c * CHUNK, CHUNK), CHUNK)
        return (
            pltpu.make_async_copy(pole_freq.at[:, cs], pf.at[:, cs], load_sem.at[c]),
            pltpu.make_async_copy(pole_amp.at[:, cs], pa.at[:, cs], load_sem.at[NCHUNK + c]),
        )

    own_l = pltpu.make_async_copy(left.at[0], lbuf.at[0], own_sem.at[0])
    own_r = pltpu.make_async_copy(right.at[0], rbuf.at[0], own_sem.at[1])
    scalar_loads = (
        pltpu.make_async_copy(freq_hbm, freq_index, own_sem.at[2]),
        pltpu.make_async_copy(energy_hbm, band_energy, own_sem.at[3]),
    )
    for copy in (own_l,) + scalar_loads:
        copy.start()
    for copy in pole_copies(0):
        copy.start()

    barrier = pltpu.get_barrier_semaphore()
    peers = [device(dc=1)]
    for k in (1, 2, 3):
        peers += [device(dx=k), device(dy=k), device(dz=k)]
    for peer in peers:
        pl.semaphore_signal(barrier, inc=1, device_id=peer, device_id_type=MESH)
    pl.semaphore_wait(barrier, len(peers))

    started = []

    def send(src, dst, send_sem, recv_sem, to):
        copy = pltpu.make_async_remote_copy(
            src_ref=src, dst_ref=dst, send_sem=send_sem, recv_sem=recv_sem,
            device_id=to, device_id_type=MESH,
        )
        copy.start()
        started.append(copy)
        return copy

    lo, hi = pl.ds(0, HALF), pl.ds(HALF, HALF)
    quarter = [pl.ds(k * (HALF // 2), HALF // 2) for k in range(4)]
    via_y, via_x = pl.ds(HALF, SHARE), pl.ds(HALF + SHARE, HALF - SHARE)
    l_at, r_at = iter(range(7)), iter(range(18))

    def send_l(src, slot, to):
        k = next(l_at)
        return send(src, lbuf.at[slot], lsend.at[k], lrecv.at[k], to)

    def send_r(source, slot, part, to):
        k = next(r_at)
        ref = right.at[0, part] if source is None else rbuf.at[source, part]
        return send(ref, rbuf.at[slot, part], rsend.at[k], rrecv.at[k], to)

    near, far = 6 - 4 * core, 2 + 4 * core
    ahead, behind = device(dz=1 + 2 * core), device(dz=3 - 2 * core)
    other, across, xup, xdown = device(dc=1), device(flip=1), device(dx=1), device(dx=3)
    l_near = send_l(left.at[0], near, ahead)
    l_c1 = send_l(left.at[0], 1, other)
    r_up = [send_r(None, 6, part, xup) for part in (lo, quarter[2])]
    r_down = [send_r(None, 2, part, xdown) for part in (hi, quarter[0])]
    r_across = [send_r(None, 1, part, across) for part in (lo, hi)]
    for k in (1, 2, 3):
        pl.semaphore_signal(plane_sem, inc=1, device_id=device(dy=k), device_id_type=MESH)
    own_r.start()
    for c in range(1, NCHUNK):
        for copy in pole_copies(c):
            copy.start()

    def scalars(slot):
        zs, cs = (z + slot // 2) % 4, (core + slot) % 2
        energy = band_energy[(zs * 2 + cs) * 2 + yhi]
        return [-4.0 + 0.25 * freq_index[w].astype(F32) - energy for w in range(2)]

    def first(slot, c):
        cs = pl.ds(pl.multiple_of(c * CHUNK, CHUNK), CHUNK)
        shifts = scalars(slot)
        for w in range(2):
            d = shifts[w] - pf[:, cs]
            screened = (pa[:, cs] * d / (d * d + 0.25)).astype(BF16)
            ubuf[slot, pl.ds(w * NST, NST), cs] = jnp.dot(
                lbuf[slot], screened, preferred_element_type=F32
            ).astype(BF16)

    def first_loop(count, slot_of, loads=False):
        def step(i, carry):
            c = i % NCHUNK
            if loads:
                @pl.when(i < NCHUNK)
                def _():
                    for copy in pole_copies(c):
                        copy.wait()
            first(slot_of(i // NCHUNK), c)
            return carry

        lax.fori_loop(0, count * NCHUNK, step, 0)

    def second(rslot):
        xs, ys = (x + rslot // 2) % 4, (ylo + rslot) % 2
        uslot = ((xs - z + 4) % 4) * 2 + (ys + core) % 2
        term = lax.dot_general(
            ubuf[uslot], rbuf[rslot], (((1,), (1,)), ((), ())), preferred_element_type=F32
        )
        for h in range(2):
            sig[pl.ds(h * 2 * NST, 2 * NST), :] += term[:, h * LANES:(h + 1) * LANES]

    def second_loop(count, slot_of):
        def step(i, carry):
            second(slot_of(i))
            return carry

        lax.fori_loop(0, count, step, 0)

    sig[...] = jnp.zeros_like(sig)
    for copy in (own_l,) + scalar_loads:
        copy.wait()
    first_loop(1, lambda i: 0, loads=True)
    l_near.wait_send()
    started.remove(l_near)
    l_far = send_l(left.at[0], far, behind)
    l_c1.wait_recv()
    first_loop(1, lambda i: 1)

    pl.semaphore_wait(plane_sem, 3)
    for k in (1, 2, 3):
        pl.semaphore_signal(all_sem, inc=1, device_id=device(dz=k), device_id_type=MESH)
    l_near.wait_recv()
    l_c2 = send_l(lbuf.at[near], near + 1, other)
    l_a = send_l(lbuf.at[near], 4, ahead)
    r_up[0].wait_recv()
    r_a = send_r(6, 4, lo, xup)
    r_up.append(send_r(None, 6, quarter[3], xup))
    r_down[0].wait_recv()
    r_b = send_r(2, 4, hi, xdown)
    r_down.append(send_r(None, 2, quarter[1], xdown))
    r_across[0].wait_recv()
    r_up_q = [send_r(1, 7, lo, xup)]
    r_down_q = [send_r(1, 3, lo, xdown)]
    first_loop(1, lambda i: near)
    l_c2.wait_recv()
    first_loop(1, lambda i: far + 1)

    r_across[1].wait_recv()
    r_up_q.append(send_r(1, 7, via_x, xup))
    r_down_q.append(send_r(1, 3, via_x, xdown))
    r_up[1].wait_recv()
    r_c = [send_r(6, 7, via_y, across), send_r(2, 3, via_y, across)]
    l_far.wait_recv()
    l_c3 = send_l(lbuf.at[far], far + 1, other)
    first_loop(1, lambda i: far)
    r_a.wait_recv()
    r_c.append(send_r(4, 5, lo, across))
    r_b.wait_recv()
    r_c.append(send_r(4, 5, hi, across))
    l_c3.wait_recv()
    first_loop(1, lambda i: near + 1)
    l_a.wait_recv()
    l_c4 = send_l(lbuf.at[4], 5, other)
    first_loop(1, lambda i: 4)
    l_c4.wait_recv()
    first_loop(1, lambda i: 5)

    own_r.wait()
    second_loop(2, lambda i: i)
    for copy in r_up[2:] + r_down[1:]:
        copy.wait_recv()
    second_loop(3, lambda i: 2 + 2 * i)
    for copy in r_up_q + r_down_q + r_c[:2]:
        copy.wait_recv()
    second_loop(2, lambda i: 3 + 4 * i)
    for copy in r_c[2:]:
        copy.wait_recv()
    second(5)

    def build(q, carry):
        base = (q // 8) * 128 + (q % 8) * 8
        for cc in range(2):
            for hh in range(2):
                at = pl.multiple_of(base + cc * 512 + hh * 64, 8)
                for r in range(2):
                    rows = pl.ds(q * 8 + cc * 4 + hh * 2 + r, 4, stride=NST)
                    tiles[pl.ds(at + 4 * r, 4), :] = sig[rows, :]
        return carry

    lax.fori_loop(0, 32, build, 0)

    def part(k, n):
        return pl.ds(pl.multiple_of(k * n, n), n)

    s = send(tiles.at[part(1 - core, 512)], in_a, ssend.at[0], srecv.at[0], other)
    pl.semaphore_wait(all_sem, 3)
    s.wait_recv()
    total[...] = tiles[part(core, 512), :] + in_a[...]

    def term(k):
        dx, dy, dz = k // 16, (k // 4) % 4, k % 4
        to = (((x + dx) % 4) * 4 + (y + dy) % 4) * 4 + (z + dz) % 4
        copy = pltpu.make_async_remote_copy(
            src_ref=total.at[part(to, 8)], dst_ref=in_f.at[part(k - 1, 8)], send_sem=ssend.at[1], recv_sem=srecv.at[1],
            device_id=device(dx=dx, dy=dy, dz=dz), device_id_type=MESH,
        )
        copy.start()

    for k in range(1, 64):
        term(k)
    every = pltpu.make_async_remote_copy(
        src_ref=total.at[pl.ds(0, 504)], dst_ref=in_f, send_sem=ssend.at[1], recv_sem=srecv.at[1],
        device_id=other, device_id_type=MESH,
    )
    me = part((x * 4 + y) * 4 + z, 8)
    every.wait_recv()
    tile = total[me, :] + jnp.sum(in_f[...].reshape(63, 8, LANES), axis=0)
    started.append(every)
    for r in range(2):
        for h in range(2):
            for w in range(2):
                at = 4 * r + 2 * h + w
                out[w, pl.ds(r, 1), pl.ds(h * LANES, LANES)] = tile[at:at + 1, :]
    for copy in started:
        copy.wait_send()


def body(freq_index, band_energy, pole_amp, pole_freq, left_pieces, right_pieces):
    anywhere = pl.BlockSpec(memory_space=pl.ANY)
    dma = pltpu.SemaphoreType.DMA
    return pl.pallas_call(
        kernel,
        out_shape=jax.ShapeDtypeStruct((2, 2, 2 * LANES), F32),
        in_specs=[anywhere] * 6,
        out_specs=pl.BlockSpec(memory_space=pltpu.VMEM),
        scratch_shapes=[
            pltpu.SMEM((2,), jnp.int32),
            pltpu.SMEM((16,), F32),
            pltpu.VMEM((TILE, TILE), F32),
            pltpu.VMEM((TILE, TILE), F32),
            pltpu.VMEM((8, NST, TILE), BF16),
            pltpu.VMEM((8, NST, TILE), BF16),
            pltpu.VMEM((8, 2 * NST, TILE), BF16),
            pltpu.VMEM((4 * NST, LANES), F32),
            pltpu.VMEM((1024, LANES), F32),
            pltpu.VMEM((512, LANES), F32),
            pltpu.VMEM((512, LANES), F32),
            pltpu.VMEM((504, LANES), F32),
            dma((2 * NCHUNK,)), dma((4,)),
            dma((7,)), dma((7,)), dma((18,)), dma((18,)), dma((2,)), dma((2,)),
            pltpu.SemaphoreType.REGULAR, pltpu.SemaphoreType.REGULAR,
        ],
        compiler_params=pltpu.CompilerParams(
            collective_id=0, has_side_effects=True, vmem_limit_bytes=56 << 20
        ),
        name="self_energy",
    )(freq_index, band_energy, pole_freq, pole_amp, left_pieces, right_pieces)


def solution(mesh):
    in_specs = (
        P(),
        P(),
        P("row", "col"),
        P("row", "col"),
        P(("col", "band"), None, "row"),
        P(("row", "band"), None, "col"),
    )
    out_specs = P(None, ("row", "col", "band"), None)
    return jax.shard_map(body, mesh=mesh, in_specs=in_specs, out_specs=out_specs, check_vma=False)
```

```python
import jax
import jax.numpy as jnp
from jax import lax
from jax.experimental import pallas as pl
from jax.experimental.pallas import tpu as pltpu
from jax.sharding import PartitionSpec as P

MESH = pl.DeviceIdType.MESH
F32 = jnp.float32
BF16 = jnp.bfloat16

NST = 256
TILE = 1024
HALF = NST // 2
LANES = 128


def kernel(freq_hbm, energy_hbm, pole_freq, pole_amp, left, right, out,
           freq_index, band_energy, pf, pa, sbuf_0, sbuf_1, lbuf, rbuf, ubuf, sig, tiles, in_a, total, in_f,
           load_sem, own_sem, lsend, lrecv, rsend, rrecv, ssend, srecv, plane_sem, all_sem):
    row, col, yhi = lax.axis_index("row"), lax.axis_index("col"), lax.axis_index("band")
    x, ylo, z, core = row // 2, row % 2, col // 2, col % 2
    y = yhi * 2 + ylo

    def device(dx=0, dy=0, dz=0, dc=0, flip=0):
        yy = (y + dy) % 4
        return {
            "row": ((x + dx) % 4) * 2 + (yy % 2 + flip) % 2,
            "col": ((z + dz) % 4) * 2 + (core + dc) % 2,
            "band": yy // 2,
        }

    own_l = pltpu.make_async_copy(left.at[0], lbuf.at[0], own_sem.at[0])
    own_r = pltpu.make_async_copy(right.at[0], rbuf.at[0], own_sem.at[1])
    scalar_loads = (
        pltpu.make_async_copy(freq_hbm, freq_index, own_sem.at[2]),
        pltpu.make_async_copy(energy_hbm, band_energy, own_sem.at[3]),
    )
    pole_loads = (
        pltpu.make_async_copy(pole_freq, pf, load_sem.at[0]),
        pltpu.make_async_copy(pole_amp, pa, load_sem.at[1]),
    )
    for copy in scalar_loads + pole_loads + (own_l, own_r):
        copy.start()

    barrier = pltpu.get_barrier_semaphore()
    peers = [device(dc=1)]
    for k in (1, 2, 3):
        peers += [device(dx=k), device(dy=k), device(dz=k)]
    for peer in peers:
        pl.semaphore_signal(barrier, inc=1, device_id=peer, device_id_type=MESH)
    pl.semaphore_wait(barrier, len(peers))

    started = []

    def plan(src, dst, send_sem, recv_sem, to):
        copy = pltpu.make_async_remote_copy(
            src_ref=src, dst_ref=dst, send_sem=send_sem, recv_sem=recv_sem,
            device_id=to, device_id_type=MESH,
        )
        started.append(copy)
        return copy

    def start(*copies):
        for copy in copies:
            copy.start()

    def arrive(*copies):
        for copy in copies:
            copy.wait_recv()

    l_at, r_at = iter(range(7)), iter(range(20))

    def plan_l(src, slot, to):
        k = next(l_at)
        return plan(src, lbuf.at[slot], lsend.at[k], lrecv.at[k], to)

    def plan_r(source, slot, begin, end, to):
        k, part = next(r_at), pl.ds(begin, end - begin)
        ref = right.at[0, part] if source is None else rbuf.at[source, part]
        return plan(ref, rbuf.at[slot, part], rsend.at[k], rrecv.at[k], to)

    near, far = 6 - 4 * core, 2 + 4 * core
    near1, far1 = near + 1, far + 1
    ahead, behind = device(dz=1 + 2 * core), device(dz=3 - 2 * core)
    other, across, xup, xdown = device(dc=1), device(flip=1), device(dx=1), device(dx=3)
    z_line = [device(dz=k) for k in (1, 2, 3)]

    l_near = plan_l(left.at[0], near, ahead)
    l_own1 = plan_l(left.at[0], 1, other)
    l_far = plan_l(left.at[0], far, behind)
    l_next = plan_l(lbuf.at[near], 4, ahead)
    l_near1 = plan_l(lbuf.at[near], near1, other)
    l_far1 = plan_l(lbuf.at[far], far1, other)
    l_five = plan_l(lbuf.at[4], 5, other)

    up = [plan_r(None, 6, begin, end, xup) for begin, end in ((0, 128), (128, 192), (192, 256))]
    down = [plan_r(None, 2, begin, end, xdown) for begin, end in ((128, 256), (0, 64), (64, 128))]
    over = [plan_r(None, 1, begin, end, across) for begin, end in ((0, 128), (128, 256))]
    up_on, down_on = plan_r(6, 4, 0, 128, xup), plan_r(2, 4, 128, 256, xdown)
    over_up = [plan_r(6, 7, begin, end, across) for begin, end in ((0, 64), (64, 96))]
    over_down = [plan_r(2, 3, begin, end, across) for begin, end in ((192, 256), (160, 192))]
    up_q, down_q = plan_r(1, 7, 96, 256, xup), plan_r(1, 3, 0, 160, xdown)
    over_on = [plan_r(4, 5, begin, end, across) for begin, end in ((64, 128), (128, 192))]
    up_far, down_far = plan_r(7, 5, 0, 64, xup), plan_r(3, 5, 192, 256, xdown)

    start(l_near, l_own1, up[0], down[0], over[0], up[1], down[1], over[1])
    for k in (1, 2, 3):
        pl.semaphore_signal(plane_sem, inc=1, device_id=device(dy=k), device_id_type=MESH)
    def scalars(slot):
        zs, cs = (z + slot // 2) % 4, (core + slot) % 2
        energy = band_energy[(zs * 2 + cs) * 2 + yhi]
        return [-4.0 + 0.25 * freq_index[w].astype(F32) - energy for w in range(2)]

    sbufs = (sbuf_0, sbuf_1)

    def screen(slot, at):
        shifts = scalars(slot)
        for w in range(2):
            d = shifts[w] - pf[...]
            sbufs[at][w] = (pa[...] * d / (d * d + 0.25)).astype(BF16)

    def first(slot, at):
        for w in range(2):
            ubuf[slot, pl.ds(w * NST, NST), :] = jnp.dot(
                lbuf[slot], sbufs[at][w], preferred_element_type=F32
            ).astype(BF16)

    def second(rslot):
        xs, ys = (x + rslot // 2) % 4, (ylo + rslot) % 2
        uslot = ((xs - z + 4) % 4) * 2 + (ys + core) % 2
        term = lax.dot_general(
            ubuf[uslot], rbuf[rslot], (((1,), (1,)), ((), ())), preferred_element_type=F32
        )
        for h in range(2):
            sig[pl.ds(h * 2 * NST, 2 * NST), :] += term[:, h * LANES:(h + 1) * LANES]

    sig[...] = jnp.zeros_like(sig)

    def at_own():
        own_l.wait()

    def at_partner():
        l_near.wait_send()
        start(l_far)
        arrive(l_own1)

    def at_near():
        arrive(up[0])
        start(up_on, up[2])
        arrive(down[0])
        start(down_on, down[2], over_up[0], over_down[0], over_up[1], over_down[1])
        arrive(l_near)
        start(l_next, l_near1)
        pl.semaphore_wait(plane_sem, 3)
        for to in z_line:
            pl.semaphore_signal(all_sem, inc=1, device_id=to, device_id_type=MESH)

    def at_far1():
        arrive(l_near1)

    def at_far():
        arrive(*over)
        start(up_q, down_q)
        arrive(l_far)
        start(l_far1)

    def at_near1():
        arrive(l_far1)
        arrive(up_on)
        start(over_on[0])
        arrive(down_on)
        start(over_on[1])
        arrive(over_up[0])
        start(up_far)

    def at_4():
        arrive(l_next)
        start(l_five)
        arrive(over_down[0])
        start(down_far)

    def at_5():
        arrive(l_five)

    heads = (at_own, at_partner, at_near, at_far1, at_far, at_near1, at_4, at_5)

    def slot_of(k):
        m = k - 2
        middle = near + ((m + m // 2) % 2) * (far - near) + m % 2
        return jnp.where(k < 2, k, jnp.where(k < 6, middle, m))

    def band_pair(pair, carry):
        for j in range(2):
            screen(slot_of(2 * pair + j), j)
        for j in range(2):
            k = 2 * pair + j
            for n in range(j, 8, 2):
                pl.when(k == n)(heads[n])
            first(slot_of(k), j)
        return carry

    for copy in scalar_loads + pole_loads:
        copy.wait()
    lax.fori_loop(0, 4, band_pair, 0)

    def at_second_0():
        own_r.wait()

    def at_second_2():
        arrive(*up[1:], *down[1:])

    def at_second_5():
        arrive(up_q, down_q, over_up[1], over_down[1])

    def at_second_7():
        arrive(*over_on, up_far, down_far)

    def second_step(i, carry):
        for n, head in ((0, at_second_0), (2, at_second_2), (5, at_second_5), (7, at_second_7)):
            pl.when(i == n)(head)
        t = i - 5
        second(jnp.where(i < 2, i, jnp.where(i < 5, 2 * (i - 1), 3 + 4 * t - 6 * (t // 2))))
        return carry

    lax.fori_loop(0, 8, second_step, 0)

    def build(q, carry):
        base = (q // 8) * 128 + (q % 8) * 8
        for cc in range(2):
            for hh in range(2):
                at = pl.multiple_of(base + cc * 512 + hh * 64, 8)
                for r in range(2):
                    rows = pl.ds(q * 8 + cc * 4 + hh * 2 + r, 4, stride=NST)
                    tiles[pl.ds(at + 4 * r, 4), :] = sig[rows, :]
        return carry

    lax.fori_loop(0, 32, build, 0)

    def part(k, n):
        return pl.ds(pl.multiple_of(k * n, n), n)

    s = plan(tiles.at[part(1 - core, 512)], in_a, ssend.at[0], srecv.at[0], other)
    s.start()
    pl.semaphore_wait(all_sem, 3)
    s.wait_recv()
    total[...] = tiles[part(core, 512), :] + in_a[...]

    def term(k):
        dx, dy, dz = k // 16, (k // 4) % 4, k % 4
        to = (((x + dx) % 4) * 4 + (y + dy) % 4) * 4 + (z + dz) % 4
        copy = pltpu.make_async_remote_copy(
            src_ref=total.at[part(to, 8)], dst_ref=in_f.at[part(k - 1, 8)], send_sem=ssend.at[1], recv_sem=srecv.at[1],
            device_id=device(dx=dx, dy=dy, dz=dz), device_id_type=MESH,
        )
        copy.start()

    for k in range(1, 64):
        term(k)
    every = pltpu.make_async_remote_copy(
        src_ref=total.at[pl.ds(0, 504)], dst_ref=in_f, send_sem=ssend.at[1], recv_sem=srecv.at[1],
        device_id=other, device_id_type=MESH,
    )
    me = part((x * 4 + y) * 4 + z, 8)
    every.wait_recv()
    tile = total[me, :] + jnp.sum(in_f[...].reshape(63, 8, LANES), axis=0)
    started.append(every)
    for r in range(2):
        for h in range(2):
            for w in range(2):
                at = 4 * r + 2 * h + w
                out[w, pl.ds(r, 1), pl.ds(h * LANES, LANES)] = tile[at:at + 1, :]
    for copy in started:
        if copy is not l_near:
            copy.wait_send()


def body(freq_index, band_energy, pole_amp, pole_freq, left_pieces, right_pieces):
    anywhere = pl.BlockSpec(memory_space=pl.ANY)
    dma = pltpu.SemaphoreType.DMA
    return pl.pallas_call(
        kernel,
        out_shape=jax.ShapeDtypeStruct((2, 2, 2 * LANES), F32),
        in_specs=[anywhere] * 6,
        out_specs=pl.BlockSpec(memory_space=pltpu.VMEM),
        scratch_shapes=[
            pltpu.SMEM((2,), jnp.int32),
            pltpu.SMEM((16,), F32),
            pltpu.VMEM((TILE, TILE), F32),
            pltpu.VMEM((TILE, TILE), F32),
            pltpu.VMEM((2, TILE, TILE), BF16),
            pltpu.VMEM((2, TILE, TILE), BF16),
            pltpu.VMEM((8, NST, TILE), BF16),
            pltpu.VMEM((8, NST, TILE), BF16),
            pltpu.VMEM((8, 2 * NST, TILE), BF16),
            pltpu.VMEM((4 * NST, LANES), F32),
            pltpu.VMEM((1024, LANES), F32),
            pltpu.VMEM((512, LANES), F32),
            pltpu.VMEM((512, LANES), F32),
            pltpu.VMEM((504, LANES), F32),
            dma((2,)), dma((4,)),
            dma((7,)), dma((7,)), dma((20,)), dma((20,)), dma((2,)), dma((2,)),
            pltpu.SemaphoreType.REGULAR, pltpu.SemaphoreType.REGULAR,
        ],
        compiler_params=pltpu.CompilerParams(
            collective_id=0, has_side_effects=True, vmem_limit_bytes=56 << 20
        ),
        name="self_energy",
    )(freq_index, band_energy, pole_freq, pole_amp, left_pieces, right_pieces)


def solution(mesh):
    in_specs = (
        P(),
        P(),
        P("row", "col"),
        P("row", "col"),
        P(("col", "band"), None, "row"),
        P(("row", "band"), None, "col"),
    )
    out_specs = P(None, ("row", "col", "band"), None)
    return jax.shard_map(body, mesh=mesh, in_specs=in_specs, out_specs=out_specs, check_vma=False)
```

```python
import jax
import jax.numpy as jnp
from jax import lax
from jax.experimental import pallas as pl
from jax.experimental.pallas import tpu as pltpu
from jax.sharding import PartitionSpec as P

MESH = pl.DeviceIdType.MESH
F32 = jnp.float32
BF16 = jnp.bfloat16

NST = 256
TILE = 1024
HALF = NST // 2
LANES = 128


def kernel(freq_hbm, energy_hbm, pole_freq, pole_amp, left, right, out,
           freq_index, band_energy, pf, pa, sbuf_0, sbuf_1, lbuf, rbuf, ubuf, sig, tiles, in_a, total, in_f,
           load_sem, own_sem, lsend, lrecv, rsend, rrecv, ssend, srecv, plane_sem, all_sem):
    row, col, yhi = lax.axis_index("row"), lax.axis_index("col"), lax.axis_index("band")
    x, ylo, z, core = row // 2, row % 2, col // 2, col % 2
    y = yhi * 2 + ylo

    def device(dx=0, dy=0, dz=0, dc=0, flip=0):
        yy = (y + dy) % 4
        return {
            "row": ((x + dx) % 4) * 2 + (yy % 2 + flip) % 2,
            "col": ((z + dz) % 4) * 2 + (core + dc) % 2,
            "band": yy // 2,
        }

    own_l = pltpu.make_async_copy(left.at[0], lbuf.at[0], own_sem.at[0])
    own_r = pltpu.make_async_copy(right.at[0], rbuf.at[0], own_sem.at[1])
    scalar_loads = (
        pltpu.make_async_copy(freq_hbm, freq_index, own_sem.at[2]),
        pltpu.make_async_copy(energy_hbm, band_energy, own_sem.at[3]),
    )
    pole_loads = (
        pltpu.make_async_copy(pole_freq, pf, load_sem.at[0]),
        pltpu.make_async_copy(pole_amp, pa, load_sem.at[1]),
    )
    for copy in scalar_loads + pole_loads + (own_l, own_r):
        copy.start()

    barrier = pltpu.get_barrier_semaphore()
    peers = [device(dc=1)]
    for k in (1, 2, 3):
        peers += [device(dx=k), device(dy=k), device(dz=k)]
    for peer in peers:
        pl.semaphore_signal(barrier, inc=1, device_id=peer, device_id_type=MESH)
    pl.semaphore_wait(barrier, len(peers))

    started = []

    def plan(src, dst, send_sem, recv_sem, to):
        copy = pltpu.make_async_remote_copy(
            src_ref=src, dst_ref=dst, send_sem=send_sem, recv_sem=recv_sem,
            device_id=to, device_id_type=MESH,
        )
        started.append(copy)
        return copy

    def start(*copies):
        for copy in copies:
            copy.start()

    def arrive(*copies):
        for copy in copies:
            copy.wait_recv()

    l_at, r_at = iter(range(7)), iter(range(20))

    def plan_l(src, slot, to):
        k = next(l_at)
        return plan(src, lbuf.at[slot], lsend.at[k], lrecv.at[k], to)

    def plan_r(source, slot, begin, end, to):
        k, part = next(r_at), pl.ds(begin, end - begin)
        ref = right.at[0, part] if source is None else rbuf.at[source, part]
        return plan(ref, rbuf.at[slot, part], rsend.at[k], rrecv.at[k], to)

    near, far = 6 - 4 * core, 2 + 4 * core
    near1, far1 = near + 1, far + 1
    ahead, behind = device(dz=1 + 2 * core), device(dz=3 - 2 * core)
    other, across, xup, xdown = device(dc=1), device(flip=1), device(dx=1), device(dx=3)
    z_line = [device(dz=k) for k in (1, 2, 3)]

    l_near = plan_l(left.at[0], near, ahead)
    l_own1 = plan_l(left.at[0], 1, other)
    l_far = plan_l(left.at[0], far, behind)
    l_next = plan_l(lbuf.at[near], 4, ahead)
    l_near1 = plan_l(lbuf.at[near], near1, other)
    l_far1 = plan_l(lbuf.at[far], far1, other)
    l_five = plan_l(lbuf.at[4], 5, other)

    up = [plan_r(None, 6, begin, end, xup) for begin, end in ((0, 128), (128, 192), (192, 256))]
    down = [plan_r(None, 2, begin, end, xdown) for begin, end in ((128, 256), (0, 64), (64, 128))]
    over = [plan_r(None, 1, begin, end, across) for begin, end in ((0, 128), (128, 256))]
    up_on, down_on = plan_r(6, 4, 0, 128, xup), plan_r(2, 4, 128, 256, xdown)
    over_up = [plan_r(6, 7, begin, end, across) for begin, end in ((0, 64), (64, 96))]
    over_down = [plan_r(2, 3, begin, end, across) for begin, end in ((192, 256), (160, 192))]
    up_q, down_q = plan_r(1, 7, 96, 256, xup), plan_r(1, 3, 0, 160, xdown)
    over_on = [plan_r(4, 5, begin, end, across) for begin, end in ((64, 128), (128, 192))]
    up_far, down_far = plan_r(7, 5, 0, 64, xup), plan_r(3, 5, 192, 256, xdown)

    start(l_near, l_own1, up[0], down[0], over[0], up[1], down[1], over[1])
    for k in (1, 2, 3):
        pl.semaphore_signal(plane_sem, inc=1, device_id=device(dy=k), device_id_type=MESH)
    def scalars(slot):
        zs, cs = (z + slot // 2) % 4, (core + slot) % 2
        energy = band_energy[(zs * 2 + cs) * 2 + yhi]
        return [-4.0 + 0.25 * freq_index[w].astype(F32) - energy for w in range(2)]

    sbufs = (sbuf_0, sbuf_1)

    def screen(slot, at):
        shifts = scalars(slot)
        for w in range(2):
            d = shifts[w] - pf[...]
            sbufs[at][w] = (pa[...] * d / (d * d + 0.25)).astype(BF16)

    def first(slot, at):
        for w in range(2):
            ubuf[slot, pl.ds(w * NST, NST), :] = jnp.dot(
                lbuf[slot], sbufs[at][w], preferred_element_type=F32
            ).astype(BF16)

    def order(i):
        t = i - 5
        return jnp.where(i < 2, i, jnp.where(i < 5, 2 * (i - 1), 3 + 4 * t - 6 * (t // 2)))

    def uslot_of(rslot):
        xs, ys = (x + rslot // 2) % 4, (ylo + rslot) % 2
        return ((xs - z + 4) % 4) * 2 + (ys + core) % 2

    def second(rslot):
        uslot = uslot_of(rslot)
        term = lax.dot_general(
            ubuf[uslot], rbuf[rslot], (((1,), (1,)), ((), ())), preferred_element_type=F32
        )
        for h in range(2):
            sig[pl.ds(h * 2 * NST, 2 * NST), :] += term[:, h * LANES:(h + 1) * LANES]

    sig[...] = jnp.zeros_like(sig)

    def at_own():
        own_l.wait()

    def at_partner():
        l_near.wait_send()
        start(l_far)
        arrive(l_own1)

    def mid_near():
        arrive(up[0])
        start(up_on, up[2])
        arrive(down[0])
        start(down_on, down[2], over_up[0], over_down[0], over_up[1], over_down[1])
        arrive(l_near)
        start(l_next, l_near1)

    def at_near():
        mid_near()
        pl.semaphore_wait(plane_sem, 3)
        for to in z_line:
            pl.semaphore_signal(all_sem, inc=1, device_id=to, device_id_type=MESH)

    def at_far1():
        arrive(l_near1)

    def mid_far():
        arrive(*over)
        start(up_q, down_q)

    def at_far():
        arrive(l_far)
        start(l_far1)

    def at_near1():
        arrive(l_far1)
        arrive(up_on)
        start(over_on[0])
        arrive(down_on)
        start(over_on[1])
        arrive(over_up[0])
        start(up_far)

    def mid_4():
        arrive(l_next)
        start(l_five)

    def at_4():
        arrive(over_down[0])
        start(down_far)

    def at_5():
        arrive(l_five)

    heads = (at_own, at_partner, at_near, at_far1, at_far, at_near1, at_4, at_5)

    def slot_of(k):
        m = k - 2
        middle = near + ((m + m // 2) % 2) * (far - near) + m % 2
        return jnp.where(k < 2, k, jnp.where(k < 6, middle, m))

    def band_pair(pair, carry):
        screen(slot_of(2 * pair), 0)
        for n, middle in ((2, mid_far), (3, mid_4)):
            pl.when(pair == n)(middle)
        screen(slot_of(2 * pair + 1), 1)
        for j in range(2):
            k = 2 * pair + j
            for n in range(j, 8, 2):
                pl.when(k == n)(heads[n])
            first(slot_of(k), j)
        return carry

    for copy in scalar_loads + pole_loads:
        copy.wait()
    lax.fori_loop(0, 4, band_pair, 0)

    def at_second_0():
        own_r.wait()

    def at_second_2():
        arrive(*up[1:], *down[1:])

    def at_second_5():
        arrive(up_q, down_q, over_up[1], over_down[1])

    def at_second_7():
        arrive(*over_on, up_far, down_far)

    def second_step(i, carry):
        for n, head in ((0, at_second_0), (2, at_second_2), (5, at_second_5), (7, at_second_7)):
            pl.when(i == n)(head)
        second(order(i))
        return carry

    lax.fori_loop(0, 8, second_step, 0)

    def build(q, carry):
        base = (q // 8) * 128 + (q % 8) * 8
        for cc in range(2):
            for hh in range(2):
                at = pl.multiple_of(base + cc * 512 + hh * 64, 8)
                for r in range(2):
                    rows = pl.ds(q * 8 + cc * 4 + hh * 2 + r, 4, stride=NST)
                    tiles[pl.ds(at + 4 * r, 4), :] = sig[rows, :]
        return carry

    lax.fori_loop(0, 32, build, 0)

    def part(k, n):
        return pl.ds(pl.multiple_of(k * n, n), n)

    s = plan(tiles.at[part(1 - core, 512)], in_a, ssend.at[0], srecv.at[0], other)
    s.start()
    pl.semaphore_wait(all_sem, 3)
    s.wait_recv()
    total[...] = tiles[part(core, 512), :] + in_a[...]

    def term(k):
        dx, dy, dz = k // 16, (k // 4) % 4, k % 4
        to = (((x + dx) % 4) * 4 + (y + dy) % 4) * 4 + (z + dz) % 4
        copy = pltpu.make_async_remote_copy(
            src_ref=total.at[part(to, 8)], dst_ref=in_f.at[part(k - 1, 8)], send_sem=ssend.at[1], recv_sem=srecv.at[1],
            device_id=device(dx=dx, dy=dy, dz=dz), device_id_type=MESH,
        )
        copy.start()

    for k in range(1, 64):
        term(k)
    every = pltpu.make_async_remote_copy(
        src_ref=total.at[pl.ds(0, 504)], dst_ref=in_f, send_sem=ssend.at[1], recv_sem=srecv.at[1],
        device_id=other, device_id_type=MESH,
    )
    me = part((x * 4 + y) * 4 + z, 8)
    every.wait_recv()
    tile = total[me, :] + jnp.sum(in_f[...].reshape(63, 8, LANES), axis=0)
    started.append(every)
    for r in range(2):
        for h in range(2):
            for w in range(2):
                at = 4 * r + 2 * h + w
                out[w, pl.ds(r, 1), pl.ds(h * LANES, LANES)] = tile[at:at + 1, :]
    for copy in started:
        if copy is not l_near:
            copy.wait_send()


def body(freq_index, band_energy, pole_amp, pole_freq, left_pieces, right_pieces):
    anywhere = pl.BlockSpec(memory_space=pl.ANY)
    dma = pltpu.SemaphoreType.DMA
    return pl.pallas_call(
        kernel,
        out_shape=jax.ShapeDtypeStruct((2, 2, 2 * LANES), F32),
        in_specs=[anywhere] * 6,
        out_specs=pl.BlockSpec(memory_space=pltpu.VMEM),
        scratch_shapes=[
            pltpu.SMEM((2,), jnp.int32),
            pltpu.SMEM((16,), F32),
            pltpu.VMEM((TILE, TILE), F32),
            pltpu.VMEM((TILE, TILE), F32),
            pltpu.VMEM((2, TILE, TILE), BF16),
            pltpu.VMEM((2, TILE, TILE), BF16),
            pltpu.VMEM((8, NST, TILE), BF16),
            pltpu.VMEM((8, NST, TILE), BF16),
            pltpu.VMEM((8, 2 * NST, TILE), BF16),
            pltpu.VMEM((4 * NST, LANES), F32),
            pltpu.VMEM((1024, LANES), F32),
            pltpu.VMEM((512, LANES), F32),
            pltpu.VMEM((512, LANES), F32),
            pltpu.VMEM((504, LANES), F32),
            dma((2,)), dma((4,)),
            dma((7,)), dma((7,)), dma((20,)), dma((20,)), dma((2,)), dma((2,)),
            pltpu.SemaphoreType.REGULAR, pltpu.SemaphoreType.REGULAR,
        ],
        compiler_params=pltpu.CompilerParams(
            collective_id=0, has_side_effects=True, vmem_limit_bytes=56 << 20
        ),
        name="self_energy",
    )(freq_index, band_energy, pole_freq, pole_amp, left_pieces, right_pieces)


def solution(mesh):
    in_specs = (
        P(),
        P(),
        P("row", "col"),
        P("row", "col"),
        P(("col", "band"), None, "row"),
        P(("row", "band"), None, "col"),
    )
    out_specs = P(None, ("row", "col", "band"), None)
    return jax.shard_map(body, mesh=mesh, in_specs=in_specs, out_specs=out_specs, check_vma=False)
```

```python
import jax
import jax.numpy as jnp
from jax import lax
from jax.experimental import pallas as pl
from jax.experimental.pallas import tpu as pltpu
from jax.sharding import PartitionSpec as P

MESH = pl.DeviceIdType.MESH
F32 = jnp.float32
BF16 = jnp.bfloat16

NST = 256
TILE = 1024
HALF = NST // 2
LANES = 128


def kernel(freq_hbm, energy_hbm, pole_freq, pole_amp, left, right, out,
           freq_index, band_energy, pf, pa, sbuf_0, sbuf_1, lbuf, rbuf, ubuf, sig, tiles, in_a, total, in_f,
           load_sem, own_sem, lsend, lrecv, rsend, rrecv, ssend, srecv, plane_sem, all_sem):
    row, col, yhi = lax.axis_index("row"), lax.axis_index("col"), lax.axis_index("band")
    x, ylo, z, core = row // 2, row % 2, col // 2, col % 2
    y = yhi * 2 + ylo

    def device(dx=0, dy=0, dz=0, dc=0, flip=0):
        yy = (y + dy) % 4
        return {
            "row": ((x + dx) % 4) * 2 + (yy % 2 + flip) % 2,
            "col": ((z + dz) % 4) * 2 + (core + dc) % 2,
            "band": yy // 2,
        }

    own_l = pltpu.make_async_copy(left.at[0], lbuf.at[0], own_sem.at[0])
    own_r = pltpu.make_async_copy(right.at[0], rbuf.at[0], own_sem.at[1])
    scalar_loads = (
        pltpu.make_async_copy(freq_hbm, freq_index, own_sem.at[2]),
        pltpu.make_async_copy(energy_hbm, band_energy, own_sem.at[3]),
    )
    pole_loads = (
        pltpu.make_async_copy(pole_freq, pf, load_sem.at[0]),
        pltpu.make_async_copy(pole_amp, pa, load_sem.at[1]),
    )
    for copy in scalar_loads + pole_loads + (own_l, own_r):
        copy.start()

    barrier = pltpu.get_barrier_semaphore()
    peers = [device(dc=1)]
    for k in (1, 2, 3):
        peers += [device(dx=k), device(dy=k), device(dz=k)]
    for peer in peers:
        pl.semaphore_signal(barrier, inc=1, device_id=peer, device_id_type=MESH)
    pl.semaphore_wait(barrier, len(peers))

    started = []

    def plan(src, dst, send_sem, recv_sem, to):
        copy = pltpu.make_async_remote_copy(
            src_ref=src, dst_ref=dst, send_sem=send_sem, recv_sem=recv_sem,
            device_id=to, device_id_type=MESH,
        )
        started.append(copy)
        return copy

    def start(*copies):
        for copy in copies:
            copy.start()

    def arrive(*copies):
        for copy in copies:
            copy.wait_recv()

    l_at, r_at = iter(range(7)), iter(range(20))

    def plan_l(src, slot, to):
        k = next(l_at)
        return plan(src, lbuf.at[slot], lsend.at[k], lrecv.at[k], to)

    def plan_r(source, slot, begin, end, to):
        k, part = next(r_at), pl.ds(begin, end - begin)
        ref = right.at[0, part] if source is None else rbuf.at[source, part]
        return plan(ref, rbuf.at[slot, part], rsend.at[k], rrecv.at[k], to)

    near, far = 6 - 4 * core, 2 + 4 * core
    near1, far1 = near + 1, far + 1
    ahead, behind = device(dz=1 + 2 * core), device(dz=3 - 2 * core)
    other, across, xup, xdown = device(dc=1), device(flip=1), device(dx=1), device(dx=3)
    z_line = [device(dz=k) for k in (1, 2, 3)]

    l_near = plan_l(left.at[0], near, ahead)
    l_own1 = plan_l(left.at[0], 1, other)
    l_far = plan_l(left.at[0], far, behind)
    l_next = plan_l(lbuf.at[near], 4, ahead)
    l_near1 = plan_l(lbuf.at[near], near1, other)
    l_far1 = plan_l(lbuf.at[far], far1, other)
    l_five = plan_l(lbuf.at[4], 5, other)

    up = [plan_r(None, 6, begin, end, xup) for begin, end in ((0, 128), (128, 192), (192, 256))]
    down = [plan_r(None, 2, begin, end, xdown) for begin, end in ((128, 256), (0, 64), (64, 128))]
    over = [plan_r(None, 1, begin, end, across) for begin, end in ((0, 128), (128, 256))]
    up_on, down_on = plan_r(6, 4, 0, 128, xup), plan_r(2, 4, 128, 256, xdown)
    over_up = [plan_r(6, 7, begin, end, across) for begin, end in ((0, 64), (64, 96))]
    over_down = [plan_r(2, 3, begin, end, across) for begin, end in ((192, 256), (160, 192))]
    up_q, down_q = plan_r(1, 7, 96, 256, xup), plan_r(1, 3, 0, 160, xdown)
    over_on = [plan_r(4, 5, begin, end, across) for begin, end in ((64, 128), (128, 192))]
    up_far, down_far = plan_r(7, 5, 0, 64, xup), plan_r(3, 5, 192, 256, xdown)

    start(l_near, l_own1, up[0], down[0], over[0], up[1], down[1], over[1])
    for k in (1, 2, 3):
        pl.semaphore_signal(plane_sem, inc=1, device_id=device(dy=k), device_id_type=MESH)
    def scalars(slot):
        zs, cs = (z + slot // 2) % 4, (core + slot) % 2
        energy = band_energy[(zs * 2 + cs) * 2 + yhi]
        return [-4.0 + 0.25 * freq_index[w].astype(F32) - energy for w in range(2)]

    sbufs = (sbuf_0, sbuf_1)

    def screen(slot, at):
        shifts = scalars(slot)
        for w in range(2):
            d = shifts[w] - pf[...]
            sbufs[at][w] = (pa[...] * d / (d * d + 0.25)).astype(BF16)

    def first(slot, at):
        for w in range(2):
            ubuf[slot, pl.ds(w * NST, NST), :] = jnp.dot(
                lbuf[slot], sbufs[at][w], preferred_element_type=F32
            ).astype(BF16)

    def order(i):
        t = i - 5
        return jnp.where(i < 2, i, jnp.where(i < 5, 2 * (i - 1), 3 + 4 * t - 6 * (t // 2)))

    def uslot_of(rslot):
        xs, ys = (x + rslot // 2) % 4, (ylo + rslot) % 2
        return ((xs - z + 4) % 4) * 2 + (ys + core) % 2

    def second(rslot):
        uslot = uslot_of(rslot)
        term = lax.dot_general(
            ubuf[uslot], rbuf[rslot], (((1,), (1,)), ((), ())), preferred_element_type=F32
        )
        for h in range(2):
            sig[pl.ds(h * 2 * NST, 2 * NST), :] += term[:, h * LANES:(h + 1) * LANES]

    sig[...] = jnp.zeros_like(sig)

    def at_own():
        own_l.wait()

    def at_partner():
        l_near.wait_send()
        start(l_far)
        arrive(l_own1)

    def mid_near():
        arrive(up[0])
        start(up_on, up[2])
        arrive(down[0])
        start(down_on, down[2], over_up[0], over_down[0], over_up[1], over_down[1])
        arrive(l_near)
        start(l_next, l_near1)

    def at_near():
        mid_near()
        pl.semaphore_wait(plane_sem, 3)
        for to in z_line:
            pl.semaphore_signal(all_sem, inc=1, device_id=to, device_id_type=MESH)

    def at_far1():
        arrive(l_near1)

    def mid_far():
        arrive(*over)
        start(up_q, down_q)

    def at_far():
        arrive(l_far)
        start(l_far1)

    def at_near1():
        arrive(l_far1)
        arrive(up_on)
        start(over_on[0])
        arrive(down_on)
        start(over_on[1])
        arrive(over_up[0])
        start(up_far)

    def mid_4():
        arrive(l_next)
        start(l_five)

    def at_4():
        arrive(over_down[0])
        start(down_far)

    def at_5():
        arrive(l_five)

    heads = (at_own, at_partner, at_near, at_far1, at_far, at_near1, at_4, at_5)

    def slot_of(k):
        m = k - 2
        middle = near + ((m + m // 2) % 2) * (far - near) + m % 2
        return jnp.where(k < 2, k, jnp.where(k < 6, middle, m))

    def band_pair(pair, carry):
        screen(slot_of(2 * pair), 0)
        for n, middle in ((2, mid_far), (3, mid_4)):
            pl.when(pair == n)(middle)
        screen(slot_of(2 * pair + 1), 1)
        for j in range(2):
            k = 2 * pair + j
            for n in range(j, 8, 2):
                pl.when(k == n)(heads[n])
            first(slot_of(k), j)
        return carry

    for copy in scalar_loads + pole_loads:
        copy.wait()
    lax.fori_loop(0, 4, band_pair, 0)

    def at_second_0():
        own_r.wait()

    def at_second_2():
        arrive(*up[1:], *down[1:])

    def at_second_5():
        arrive(up_q, down_q, over_up[1], over_down[1])

    def at_second_7():
        arrive(*over_on, up_far, down_far)

    def second_step(i, carry):
        for n, head in ((0, at_second_0), (2, at_second_2), (5, at_second_5), (7, at_second_7)):
            pl.when(i == n)(head)
        second(order(i))
        return carry

    lax.fori_loop(0, 8, second_step, 0)

    def build(q, carry):
        base = (q // 8) * 128 + (q % 8) * 8
        for cc in range(2):
            for hh in range(2):
                at = pl.multiple_of(base + cc * 512 + hh * 64, 8)
                for r in range(2):
                    rows = pl.ds(q * 8 + cc * 4 + hh * 2 + r, 4, stride=NST)
                    tiles[pl.ds(at + 4 * r, 4), :] = sig[rows, :]
        return carry

    lax.fori_loop(0, 32, build, 0)

    def part(k, n):
        return pl.ds(pl.multiple_of(k * n, n), n)

    s = plan(tiles.at[part(1 - core, 512)], in_a, ssend.at[0], srecv.at[0], other)
    s.start()
    pl.semaphore_wait(all_sem, 3)
    s.wait_recv()
    in_a[...] = tiles[part(core, 512), :] + in_a[...]
    total[...] = in_a[...].reshape(64, 8, LANES).astype(BF16)

    def term(k):
        dx, dy, dz = k // 16, (k // 4) % 4, k % 4
        to = (((x + dx) % 4) * 4 + (y + dy) % 4) * 4 + (z + dz) % 4
        copy = pltpu.make_async_remote_copy(
            src_ref=total.at[to], dst_ref=in_f.at[k - 1], send_sem=ssend.at[1], recv_sem=srecv.at[1],
            device_id=device(dx=dx, dy=dy, dz=dz), device_id_type=MESH,
        )
        copy.start()

    for k in range(1, 64):
        term(k)
    every = pltpu.make_async_remote_copy(
        src_ref=total.at[pl.ds(0, 63)], dst_ref=in_f, send_sem=ssend.at[1], recv_sem=srecv.at[1],
        device_id=other, device_id_type=MESH,
    )
    me = part((x * 4 + y) * 4 + z, 8)
    every.wait_recv()
    tile = in_a[me, :] + jnp.sum(in_f[...].astype(F32), axis=0)
    started.append(every)
    for r in range(2):
        for h in range(2):
            for w in range(2):
                at = 4 * r + 2 * h + w
                out[w, pl.ds(r, 1), pl.ds(h * LANES, LANES)] = tile[at:at + 1, :]
    for copy in started:
        if copy is not l_near:
            copy.wait_send()


def body(freq_index, band_energy, pole_amp, pole_freq, left_pieces, right_pieces):
    anywhere = pl.BlockSpec(memory_space=pl.ANY)
    dma = pltpu.SemaphoreType.DMA
    return pl.pallas_call(
        kernel,
        out_shape=jax.ShapeDtypeStruct((2, 2, 2 * LANES), F32),
        in_specs=[anywhere] * 6,
        out_specs=pl.BlockSpec(memory_space=pltpu.VMEM),
        scratch_shapes=[
            pltpu.SMEM((2,), jnp.int32),
            pltpu.SMEM((16,), F32),
            pltpu.VMEM((TILE, TILE), F32),
            pltpu.VMEM((TILE, TILE), F32),
            pltpu.VMEM((2, TILE, TILE), BF16),
            pltpu.VMEM((2, TILE, TILE), BF16),
            pltpu.VMEM((8, NST, TILE), BF16),
            pltpu.VMEM((8, NST, TILE), BF16),
            pltpu.VMEM((8, 2 * NST, TILE), BF16),
            pltpu.VMEM((4 * NST, LANES), F32),
            pltpu.VMEM((1024, LANES), F32),
            pltpu.VMEM((512, LANES), F32),
            pltpu.VMEM((64, 8, LANES), BF16),
            pltpu.VMEM((63, 8, LANES), BF16),
            dma((2,)), dma((4,)),
            dma((7,)), dma((7,)), dma((20,)), dma((20,)), dma((2,)), dma((2,)),
            pltpu.SemaphoreType.REGULAR, pltpu.SemaphoreType.REGULAR,
        ],
        compiler_params=pltpu.CompilerParams(
            collective_id=0, has_side_effects=True, vmem_limit_bytes=56 << 20
        ),
        name="self_energy",
    )(freq_index, band_energy, pole_freq, pole_amp, left_pieces, right_pieces)


def solution(mesh):
    in_specs = (
        P(),
        P(),
        P("row", "col"),
        P("row", "col"),
        P(("col", "band"), None, "row"),
        P(("row", "band"), None, "col"),
    )
    out_specs = P(None, ("row", "col", "band"), None)
    return jax.shard_map(body, mesh=mesh, in_specs=in_specs, out_specs=out_specs, check_vma=False)
```

```python
import jax
import jax.numpy as jnp
from jax import lax
from jax.experimental import pallas as pl
from jax.experimental.pallas import tpu as pltpu
from jax.sharding import PartitionSpec as P

MESH = pl.DeviceIdType.MESH
F32 = jnp.float32
BF16 = jnp.bfloat16

NST = 256
TILE = 1024
HALF = NST // 2
LANES = 128


def kernel(freq_hbm, energy_hbm, pole_freq, pole_amp, left, right, out,
           freq_index, band_energy, pf, pa, sbuf_0, sbuf_1, lbuf, rbuf, ubuf, sig, tiles, in_a, total, in_f,
           load_sem, own_sem, lsend, lrecv, rsend, rrecv, ssend, srecv, plane_sem, all_sem):
    row, col, yhi = lax.axis_index("row"), lax.axis_index("col"), lax.axis_index("band")
    x, ylo, z, core = row // 2, row % 2, col // 2, col % 2
    y = yhi * 2 + ylo

    def device(dx=0, dy=0, dz=0, dc=0, flip=0):
        yy = (y + dy) % 4
        return {
            "row": ((x + dx) % 4) * 2 + (yy % 2 + flip) % 2,
            "col": ((z + dz) % 4) * 2 + (core + dc) % 2,
            "band": yy // 2,
        }

    own_l = pltpu.make_async_copy(left.at[0], lbuf.at[0], own_sem.at[0])
    own_r = pltpu.make_async_copy(right.at[0], rbuf.at[0], own_sem.at[1])
    scalar_loads = (
        pltpu.make_async_copy(freq_hbm, freq_index, own_sem.at[2]),
        pltpu.make_async_copy(energy_hbm, band_energy, own_sem.at[3]),
    )
    pole_loads = (
        pltpu.make_async_copy(pole_freq, pf, load_sem.at[0]),
        pltpu.make_async_copy(pole_amp, pa, load_sem.at[1]),
    )
    for copy in scalar_loads + pole_loads + (own_l, own_r):
        copy.start()

    barrier = pltpu.get_barrier_semaphore()
    peers = [device(dc=1)]
    for k in (1, 2, 3):
        peers += [device(dx=k), device(dy=k), device(dz=k)]
    for peer in peers:
        pl.semaphore_signal(barrier, inc=1, device_id=peer, device_id_type=MESH)
    pl.semaphore_wait(barrier, len(peers))

    started = []

    def plan(src, dst, send_sem, recv_sem, to):
        copy = pltpu.make_async_remote_copy(
            src_ref=src, dst_ref=dst, send_sem=send_sem, recv_sem=recv_sem,
            device_id=to, device_id_type=MESH,
        )
        started.append(copy)
        return copy

    def start(*copies):
        for copy in copies:
            copy.start()

    def arrive(*copies):
        for copy in copies:
            copy.wait_recv()

    l_at, r_at = iter(range(7)), iter(range(20))

    def plan_l(src, slot, to):
        k = next(l_at)
        return plan(src, lbuf.at[slot], lsend.at[k], lrecv.at[k], to)

    def plan_r(source, slot, begin, end, to):
        k, part = next(r_at), pl.ds(begin, end - begin)
        ref = right.at[0, part] if source is None else rbuf.at[source, part]
        return plan(ref, rbuf.at[slot, part], rsend.at[k], rrecv.at[k], to)

    near, far = 6 - 4 * core, 2 + 4 * core
    near1, far1 = near + 1, far + 1
    ahead, behind = device(dz=1 + 2 * core), device(dz=3 - 2 * core)
    other, across, xup, xdown = device(dc=1), device(flip=1), device(dx=1), device(dx=3)
    z_line = [device(dz=k) for k in (1, 2, 3)]

    l_near = plan_l(left.at[0], near, ahead)
    l_own1 = plan_l(left.at[0], 1, other)
    l_far = plan_l(left.at[0], far, behind)
    l_next = plan_l(lbuf.at[near], 4, ahead)
    l_near1 = plan_l(lbuf.at[near], near1, other)
    l_far1 = plan_l(lbuf.at[far], far1, other)
    l_five = plan_l(lbuf.at[4], 5, other)

    up = [plan_r(None, 6, begin, end, xup) for begin, end in ((0, 128), (128, 192), (192, 256))]
    down = [plan_r(None, 2, begin, end, xdown) for begin, end in ((128, 256), (0, 64), (64, 128))]
    over = [plan_r(None, 1, begin, end, across) for begin, end in ((0, 128), (128, 256))]
    up_on, down_on = plan_r(6, 4, 0, 128, xup), plan_r(2, 4, 128, 256, xdown)
    over_up = [plan_r(6, 7, begin, end, across) for begin, end in ((0, 64), (64, 96))]
    over_down = [plan_r(2, 3, begin, end, across) for begin, end in ((192, 256), (160, 192))]
    up_q, down_q = plan_r(1, 7, 96, 256, xup), plan_r(1, 3, 0, 160, xdown)
    over_on = [plan_r(4, 5, begin, end, across) for begin, end in ((64, 128), (128, 192))]
    up_far, down_far = plan_r(7, 5, 0, 64, xup), plan_r(3, 5, 192, 256, xdown)

    start(l_near, l_own1, up[0], down[0], over[0], up[1], down[1], over[1])
    for k in (1, 2, 3):
        pl.semaphore_signal(plane_sem, inc=1, device_id=device(dy=k), device_id_type=MESH)
    def scalars(slot):
        zs, cs = (z + slot // 2) % 4, (core + slot) % 2
        energy = band_energy[(zs * 2 + cs) * 2 + yhi]
        return [-4.0 + 0.25 * freq_index[w].astype(F32) - energy for w in range(2)]

    sbufs = (sbuf_0, sbuf_1)

    def screen(slot, at):
        shifts = scalars(slot)
        for w in range(2):
            d = shifts[w] - pf[...]
            sbufs[at][w] = (pa[...] * d / (d * d + 0.25)).astype(BF16)

    def first(slot, at):
        for w in range(2):
            ubuf[slot, pl.ds(w * NST, NST), :] = jnp.dot(
                lbuf[slot], sbufs[at][w], preferred_element_type=F32
            ).astype(BF16)

    def order(i):
        t = i - 5
        return jnp.where(i < 2, i, jnp.where(i < 5, 2 * (i - 1), 3 + 4 * t - 6 * (t // 2)))

    def uslot_of(rslot):
        xs, ys = (x + rslot // 2) % 4, (ylo + rslot) % 2
        return ((xs - z + 4) % 4) * 2 + (ys + core) % 2

    def second(rslot):
        uslot = uslot_of(rslot)
        term = lax.dot_general(
            ubuf[uslot], rbuf[rslot], (((1,), (1,)), ((), ())), preferred_element_type=F32
        )
        for h in range(2):
            sig[pl.ds(h * 2 * NST, 2 * NST), :] += term[:, h * LANES:(h + 1) * LANES]

    sig[...] = jnp.zeros_like(sig)

    def at_own():
        own_l.wait()

    def at_partner():
        l_near.wait_send()
        start(l_far)
        arrive(l_own1)

    def mid_near():
        arrive(up[0])
        start(up_on, up[2])
        arrive(down[0])
        start(down_on, down[2], over_up[0], over_down[0], over_up[1], over_down[1])
        arrive(l_near)
        start(l_next, l_near1)

    def at_near():
        mid_near()
        pl.semaphore_wait(plane_sem, 3)
        for to in z_line:
            pl.semaphore_signal(all_sem, inc=1, device_id=to, device_id_type=MESH)

    def at_far1():
        arrive(l_near1)

    def mid_far():
        arrive(*over)
        start(up_q, down_q)

    def at_far():
        arrive(l_far)
        start(l_far1)

    def at_near1():
        arrive(l_far1)
        arrive(up_on)
        start(over_on[0])
        arrive(down_on)
        start(over_on[1])
        arrive(over_up[0])
        start(up_far)

    def mid_4():
        arrive(l_next)
        start(l_five)

    def at_4():
        arrive(over_down[0])
        start(down_far)

    def at_5():
        arrive(l_five)

    heads = (at_own, at_partner, at_near, at_far1, at_far, at_near1, at_4, at_5)

    def slot_of(k):
        m = k - 2
        middle = near + ((m + m // 2) % 2) * (far - near) + m % 2
        return jnp.where(k < 2, k, jnp.where(k < 6, middle, m))

    def band_pair(pair, carry):
        screen(slot_of(2 * pair), 0)
        for n, middle in ((2, mid_far), (3, mid_4)):
            pl.when(pair == n)(middle)
        screen(slot_of(2 * pair + 1), 1)
        for j in range(2):
            k = 2 * pair + j
            for n in range(j, 8, 2):
                pl.when(k == n)(heads[n])
            first(slot_of(k), j)
        return carry

    for copy in scalar_loads + pole_loads:
        copy.wait()
    lax.fori_loop(0, 4, band_pair, 0)

    def at_second_0():
        own_r.wait()

    def at_second_2():
        arrive(*up[1:], *down[1:])

    def at_second_5():
        arrive(up_q, down_q, over_up[1], over_down[1])

    def at_second_7():
        arrive(*over_on, up_far, down_far)

    def second_step(i, carry):
        for n, head in ((0, at_second_0), (2, at_second_2), (5, at_second_5), (7, at_second_7)):
            pl.when(i == n)(head)
        second(order(i))
        return carry

    lax.fori_loop(0, 8, second_step, 0)

    def build(q, carry):
        base = (q // 8) * 128 + (q % 8) * 8
        for cc in range(2):
            for hh in range(2):
                at = pl.multiple_of(base + cc * 512 + hh * 64, 8)
                for r in range(2):
                    rows = pl.ds(q * 8 + cc * 4 + hh * 2 + r, 4, stride=NST)
                    tiles[pl.ds(at + 4 * r, 4), :] = sig[rows, :]
        return carry

    lax.fori_loop(0, 32, build, 0)

    def part(k, n):
        return pl.ds(pl.multiple_of(k * n, n), n)

    s = plan(tiles.at[part(1 - core, 512)], in_a, ssend.at[0], srecv.at[0], other)
    s.start()
    pl.semaphore_wait(all_sem, 3)
    s.wait_recv()
    in_a[...] = tiles[part(core, 512), :] + in_a[...]
    total[...] = in_a[...].reshape(64, 8, LANES).astype(BF16)

    def term(k):
        dx, dy, dz = k // 16, (k // 4) % 4, k % 4
        to = (((x + dx) % 4) * 4 + (y + dy) % 4) * 4 + (z + dz) % 4
        copy = pltpu.make_async_remote_copy(
            src_ref=total.at[to], dst_ref=in_f.at[k - 1], send_sem=ssend.at[1], recv_sem=srecv.at[1],
            device_id=device(dx=dx, dy=dy, dz=dz), device_id_type=MESH,
        )
        copy.start()

    def hops(k):
        return sum(min(d, 4 - d) for d in (k // 16, (k // 4) % 4, k % 4))

    for k in sorted(range(1, 64), key=hops, reverse=True):
        term(k)
    every = pltpu.make_async_remote_copy(
        src_ref=total.at[pl.ds(0, 63)], dst_ref=in_f, send_sem=ssend.at[1], recv_sem=srecv.at[1],
        device_id=other, device_id_type=MESH,
    )
    me = part((x * 4 + y) * 4 + z, 8)
    every.wait_recv()
    tile = in_a[me, :] + jnp.sum(in_f[...].astype(F32), axis=0)
    started.append(every)
    for r in range(2):
        for h in range(2):
            for w in range(2):
                at = 4 * r + 2 * h + w
                out[w, pl.ds(r, 1), pl.ds(h * LANES, LANES)] = tile[at:at + 1, :]
    for copy in started:
        if copy is not l_near:
            copy.wait_send()


def body(freq_index, band_energy, pole_amp, pole_freq, left_pieces, right_pieces):
    anywhere = pl.BlockSpec(memory_space=pl.ANY)
    dma = pltpu.SemaphoreType.DMA
    return pl.pallas_call(
        kernel,
        out_shape=jax.ShapeDtypeStruct((2, 2, 2 * LANES), F32),
        in_specs=[anywhere] * 6,
        out_specs=pl.BlockSpec(memory_space=pltpu.VMEM),
        scratch_shapes=[
            pltpu.SMEM((2,), jnp.int32),
            pltpu.SMEM((16,), F32),
            pltpu.VMEM((TILE, TILE), F32),
            pltpu.VMEM((TILE, TILE), F32),
            pltpu.VMEM((2, TILE, TILE), BF16),
            pltpu.VMEM((2, TILE, TILE), BF16),
            pltpu.VMEM((8, NST, TILE), BF16),
            pltpu.VMEM((8, NST, TILE), BF16),
            pltpu.VMEM((8, 2 * NST, TILE), BF16),
            pltpu.VMEM((4 * NST, LANES), F32),
            pltpu.VMEM((1024, LANES), F32),
            pltpu.VMEM((512, LANES), F32),
            pltpu.VMEM((64, 8, LANES), BF16),
            pltpu.VMEM((63, 8, LANES), BF16),
            dma((2,)), dma((4,)),
            dma((7,)), dma((7,)), dma((20,)), dma((20,)), dma((2,)), dma((2,)),
            pltpu.SemaphoreType.REGULAR, pltpu.SemaphoreType.REGULAR,
        ],
        compiler_params=pltpu.CompilerParams(
            collective_id=0, has_side_effects=True, vmem_limit_bytes=56 << 20
        ),
        name="self_energy",
    )(freq_index, band_energy, pole_freq, pole_amp, left_pieces, right_pieces)


def solution(mesh):
    in_specs = (
        P(),
        P(),
        P("row", "col"),
        P("row", "col"),
        P(("col", "band"), None, "row"),
        P(("row", "band"), None, "col"),
    )
    out_specs = P(None, ("row", "col", "band"), None)
    return jax.shard_map(body, mesh=mesh, in_specs=in_specs, out_specs=out_specs, check_vma=False)
```
